32 devices in a mesh: gx: 2 (over y), gy: 4 (over z), gz: 4 (over x, core).
Axes of the slice: x: 2, y: 2, z: 4, core: 2. Of those that a mesh axis runs over, the one named last changes fastest.
Arguments:
- moments: float32 [32, 128, 16, 128], P('gx', ('gy', 'gz')), may hold values from -128 to 128, as said below
- stiffness: float32 [32, 128, 16], P('gx', ('gy', 'gz')), may hold values from 0.5 to 4
- damping: float32 [32, 128, 16], P('gx', ('gy', 'gz')), may hold values from 0.05 to 1
- density: float32 [32, 128, 16], P('gx', ('gy', 'gz')), may hold values from 0.5 to 1.5
- ritz_coeffs: float32 [128, 128], replicated, may hold values from -128 to 128
- shifts: float32 [128], replicated, may hold values from -1.5 to -0.3
Outputs:
- ritz_vectors: float32 [32, 128, 16, 128], P('gx', ('gy', 'gz'))
- ritz_residual: float32 [32, 128, 16, 128], P('gx', ('gy', 'gz'))
- stiff_proj: float32 [128, 128], replicated
- damp_proj: float32 [128, 128], replicated
- mass_proj: float32 [128, 128], replicated
- first_factor: float32 [128, 128], replicated
The draws below stay inside these ranges and needn't reach their ends.
Inputs may be any that keep to these rules, and one draw needn't show every extreme that they name: `moments`: A real block of full column rank.
All inputs are finite; a program needn't handle non-finite values.
Results may differ from the reference program's by a relative error of at most 0.0004.
Values sent between devices are 32-bit elements; how exact they have to be, the bound alone decides.
A program may use at most 64 MiB of HBM per device.

```python
import math
import jax
import jax.numpy as jnp
from jax import lax

COLS = 128
NZ = 16
NX = 32
NY = 128


def draw_moments(key, part):
    key_own = jax.random.fold_in(key, 11)
    key_common = jax.random.fold_in(key, 23)
    key_scale = jax.random.fold_in(key, 37)
    own = jax.random.truncated_normal(key_own, -4.0, 4.0, (NX, NY, NZ, COLS), jnp.float32)
    common = jax.random.truncated_normal(key_common, -4.0, 4.0, (NX, NY, NZ, 1), jnp.float32)
    scales = jnp.exp(jax.random.uniform(key_scale, (COLS,), jnp.float32, 0.0, math.log(10.0)))
    weight_own = 0.01
    ramp = 1.0 + 2.0 * jnp.arange(NX, dtype=jnp.float32) / (NX - 1)
    return ramp.reshape(NX, 1, 1, 1) * scales * (common + weight_own * own)


def steps_of(stream_key, extent, pieces, low, largest):
    loudness, own = 1.0, jax.random.fold_in(stream_key, 6)
    for dim, parts in pieces:
        draws = jnp.exp(jax.random.uniform(jax.random.fold_in(own, dim), (parts,), jnp.float32, low / len(pieces), largest / len(pieces)))
        loudness = loudness * jnp.repeat(draws, extent[dim] // parts).reshape([-1 if axis == dim else 1 for axis in range(len(extent))])
    return loudness


def centred(key, shape, width, reach, kind=jnp.bfloat16):
    return jnp.clip(width * jax.random.normal(key, shape, jnp.float32), -reach, reach).astype(kind)


def setup_inputs(seed: int = 0) -> dict:
    splits = jax.random.split(jax.random.key(seed), 7)
    moments = draw_moments(jax.random.fold_in(splits[6], 71), 0)
    stiffness = jnp.clip(jnp.exp(math.log(4.0) - 2.0794415 * jax.random.uniform(splits[1], (NX, NY, NZ), jnp.float32) ** steps_of(splits[1], (NX, NY, NZ), ((0, 2), (1, 16)), -0.2, 0.2)), 0.5, 4.0)
    damping = jnp.clip(jnp.exp(math.log(1.0) - 2.9957323 * jax.random.uniform(splits[2], (NX, NY, NZ), jnp.float32) ** steps_of(splits[2], (NX, NY, NZ), ((0, 2), (1, 16)), -0.2, 0.2)), 0.05, 1.0)
    density = jnp.clip(0.5 + 1.0 * jax.random.uniform(splits[3], (NX, NY, NZ), jnp.float32) ** steps_of(splits[3], (NX, NY, NZ), ((0, 2), (1, 16)), -0.2, 0.2), 0.5, 1.5)
    ritz_coeffs = centred(splits[4], (COLS, COLS), ((NX * NY * NZ / COLS) ** 0.5), 128.0, jnp.float32)
    shifts = jnp.clip(jax.random.uniform(splits[5], (COLS,), jnp.float32, -1.5, -0.3), -1.5, -0.3)
    return dict(moments=moments, stiffness=stiffness, damping=damping, density=density, ritz_coeffs=ritz_coeffs, shifts=shifts)


def factorize(gram):
    count = gram.shape[0]
    index = jnp.arange(count, dtype=jnp.int32)

    def column_step(j, carry):
        work, lower = carry
        onehot = (index == j).astype(gram.dtype)
        column = lax.optimization_barrier(jnp.sum(work * onehot[None, :], axis=1))
        pivot = jnp.sum(column * onehot)
        column = jnp.where(index >= j, column, jnp.zeros_like(column)) / jnp.sqrt(pivot)
        lower = lower + column[:, None] * onehot[None, :]
        work = work - column[:, None] * column[None, :]
        return (work, lower)
    start = (gram, jnp.zeros_like(gram))
    lower = lax.fori_loop(0, count, column_step, start)[1]

    def row_step(i, inverse):
        onehot = (index == i).astype(gram.dtype)
        row = lax.optimization_barrier(jnp.sum(lower * onehot[:, None], axis=0))
        pivot = jnp.sum(row * onehot)
        rhs = onehot - lax.optimization_barrier(jnp.sum(row[:, None] * inverse, axis=0))
        return inverse + onehot[:, None] * (rhs / pivot)[None, :]
    inverse = lax.fori_loop(0, count, row_step, jnp.zeros_like(gram))
    return (lower, inverse.T)

def neighbours(field):
    padded = jnp.pad(field, ((1, 1), (1, 1), (1, 1), (0, 0)))
    total = padded[2:, 1:-1, 1:-1] + padded[:-2, 1:-1, 1:-1]
    total = total + padded[1:-1, 2:, 1:-1] + padded[1:-1, :-2, 1:-1]
    total = total + padded[1:-1, 1:-1, 2:] + padded[1:-1, 1:-1, :-2]
    return total

def reference(moments, stiffness, damping, density, ritz_coeffs, shifts):
    highest = lax.Precision.HIGHEST
    cells = NX * NY * NZ
    flat = moments.reshape(cells, COLS)
    lower_one, first_inv = factorize(jnp.dot(flat.T, flat, precision=highest))
    first_factor = lower_one.T / jnp.sqrt(jnp.float32(cells))
    basis_one = jnp.dot(flat, first_inv, precision=highest)
    second_inv = factorize(jnp.dot(basis_one.T, basis_one, precision=highest))[1]
    basis = jnp.dot(basis_one, second_inv, precision=highest)
    near = neighbours(basis.reshape(NX, NY, NZ, COLS)).reshape(cells, COLS)
    stiff_col = stiffness.reshape(cells, 1)
    damp_col = damping.reshape(cells, 1)
    dens_col = density.reshape(cells, 1)
    k_block = (6.0 + stiff_col) * basis - near
    c_block = damp_col * basis
    m_block = dens_col * basis + near / 12.0
    stiff_proj = jnp.dot(basis.T, k_block, precision=highest)
    damp_proj = jnp.dot(basis.T, c_block, precision=highest)
    mass_proj = jnp.dot(basis.T, m_block, precision=highest)
    ritz = jnp.dot(basis, ritz_coeffs, precision=highest)
    resid = jnp.dot(k_block, ritz_coeffs, precision=highest)
    resid = resid + jnp.dot(c_block, ritz_coeffs, precision=highest) * shifts
    resid = resid + jnp.dot(m_block, ritz_coeffs, precision=highest) * (shifts * shifts)
    return (ritz.reshape(NX, NY, NZ, COLS), resid.reshape(NX, NY, NZ, COLS), stiff_proj, damp_proj, mass_proj, first_factor)
```

```python
import functools
import math
import jax
import jax.numpy as jnp
from jax import lax
from jax.experimental import pallas as pl
from jax.experimental.pallas import tpu as pltpu
from jax.sharding import PartitionSpec as P

MESH = pl.DeviceIdType.MESH
HI = lax.Precision.HIGHEST
F32 = jnp.float32
BLK = 8


def mm(a, b):
    return lax.dot_general(a, b, (((1,), (0,)), ((), ())), precision=HI, preferred_element_type=F32)


def mm_t(a, b):
    return lax.dot_general(a, b, (((0,), (0,)), ((), ())), precision=HI, preferred_element_type=F32)


def factorize(work, upper, inverse):
    n = work.shape[0]
    lane = lax.broadcasted_iota(jnp.int32, (BLK, n), 1)
    sub = lax.broadcasted_iota(jnp.int32, (BLK, n), 0)
    lane_all = lax.broadcasted_iota(jnp.int32, (n, n), 1)

    def block(jb, carry):
        first = pl.multiple_of(jb * BLK, BLK)
        rows = work[pl.ds(first, BLK), :]
        cols = [
            jnp.broadcast_to(
                jnp.sum(jnp.where(lane == first + k, rows, 0.0), axis=1, keepdims=True), (BLK, n)
            )
            for k in range(BLK)
        ]
        u = jnp.where(lane >= first, rows, 0.0)
        e = jnp.where(lane < first, rows, jnp.where(lane == first + sub, 1.0, 0.0))
        pivots = jnp.zeros((BLK, n), F32)
        for s in range(BLK):
            pivot = jnp.broadcast_to(cols[s][s : s + 1], (BLK, n))
            pivots = jnp.where(sub == s, pivot, pivots)
            if s == BLK - 1:
                break
            m = jnp.where(sub > s, cols[s] / pivot, 0.0)
            for k in range(s + 1, BLK):
                cols[k] = cols[k] - m * cols[k][s : s + 1]
            u = u - m * u[s : s + 1]
            e = e - m * e[s : s + 1]
        scale = 1.0 / jnp.sqrt(pivots)
        u = jnp.where(lane >= first + sub, u * scale, 0.0)
        e = e * scale
        upper[pl.ds(first, BLK), :] = u
        inverse[pl.ds(first, BLK), :] = e
        beyond = jnp.where(lane >= first + BLK, u, 0.0)
        panel = (lane_all >= first) & (lane_all < first + BLK)
        work[...] = jnp.where(panel, 0.0, work[...]) - mm_t(beyond, beyond + e)
        return carry

    lax.fori_loop(0, n // BLK, block, 0)


def kernel(
    sizes,
    y_ref, fields_ref, ritz_ref, shifts_ref,
    vec_ref, res_ref, stiff_ref, damp_ref, mass_ref, factor_ref,
    pad, halo_x, halo_y, work, upper, inv_a, inv_b,
    g_src, g_recv, g_z, g_full, h_recv, h_z, h_full, p_src, p_recv, p_z, p_full, h_src, proj,
    halo_send, halo_got, a_send, a_got, z_send, z_got, b_send, b_got,
):
    nx, ny, nz, all_cells = sizes
    bx, by, bz, w = y_ref.shape
    group = nx * nz
    ix, iy, iz = lax.axis_index("gx"), lax.axis_index("gy"), lax.axis_index("gz")
    mine = ix * nz + iz
    line = iy * nz + iz

    def group_id(a):
        return (lax.div(a, nz), iy, lax.rem(a, nz))

    def line_id(a):
        return (ix, lax.div(a, nz), lax.rem(a, nz))

    sides = [
        (ix > 0, (ix - 1, iy, iz), y_ref.at[0], halo_x.at[1], halo_x.at[0]),
        (ix < nx - 1, (ix + 1, iy, iz), y_ref.at[bx - 1], halo_x.at[0], halo_x.at[1]),
        (line > 0, line_id(line - 1), y_ref.at[:, 0], halo_y.at[1], halo_y.at[0]),
        (line < ny * nz - 1, line_id(line + 1), y_ref.at[:, by - 1], halo_y.at[0], halo_y.at[1]),
    ]
    peers = [lax.rem(mine + d, group) for d in range(1, group)]
    planes = [lax.rem(iy + d, ny) for d in range(1, ny)]

    barrier = pltpu.get_barrier_semaphore()
    for peer in peers:
        pl.semaphore_signal(barrier, inc=1, device_id=group_id(peer), device_id_type=MESH)
    for plane in planes:
        pl.semaphore_signal(barrier, inc=1, device_id=(ix, plane, iz), device_id_type=MESH)
    for exists, device, _, _, _ in sides:
        @pl.when(exists)
        def _():
            pl.semaphore_signal(barrier, inc=1, device_id=device, device_id_type=MESH)

    def gram_step(i, total):
        rows = y_ref[pl.ds(i * 4, 4)].reshape(4 * by * bz, w)
        return total + mm_t(rows, rows)

    work[...] = lax.fori_loop(0, bx // 4, gram_step, jnp.zeros((w, w), F32))

    beside = sum(exists.astype(jnp.int32) for exists, _, _, _, _ in sides)
    pl.semaphore_wait(barrier, group - 1 + ny - 1 + beside)

    def halo_copy(k):
        _, device, src, dst, _ = sides[k]
        other = k ^ 1
        return pltpu.make_async_remote_copy(
            src_ref=src, dst_ref=dst, send_sem=halo_send.at[k], recv_sem=halo_got.at[other],
            device_id=device, device_id_type=MESH,
        )

    def scatter_start(slot, src, recv):
        copies = []
        for d, peer in enumerate(peers):
            copy = pltpu.make_async_remote_copy(
                src_ref=src.at[peer], dst_ref=recv.at[d], send_sem=a_send.at[slot, d],
                recv_sem=a_got.at[slot, d], device_id=group_id(peer), device_id_type=MESH,
            )
            copy.start()
            copies.append(copy)
        return copies

    def plane_start(slot, copies, src, recv, z):
        for copy in copies:
            copy.wait_recv()
        total = src[mine]
        for d in range(group - 1):
            total = total + recv[d]
        z[iy] = total
        after = []
        for d, plane in enumerate(planes):
            copy = pltpu.make_async_remote_copy(
                src_ref=z.at[iy], dst_ref=z.at[iy], send_sem=z_send.at[slot, d],
                recv_sem=z_got.at[slot, d], device_id=(ix, plane, iz), device_id_type=MESH,
            )
            copy.start()
            after.append(copy)
        return after

    def gather_start(slot, copies, z, full):
        for copy in copies:
            copy.wait_recv()
        total = z[0]
        for d in range(1, ny):
            total = total + z[d]
        full[mine] = total
        after = []
        for d, peer in enumerate(peers):
            copy = pltpu.make_async_remote_copy(
                src_ref=full.at[mine], dst_ref=full.at[mine], send_sem=b_send.at[slot, d],
                recv_sem=b_got.at[slot, d], device_id=group_id(peer), device_id_type=MESH,
            )
            copy.start()
            after.append(copy)
        return after

    def gather_end(copies, full, out):
        for copy in copies:
            copy.wait_recv()
        r = full.shape[1]
        for a in range(group):
            out[a * r : (a + 1) * r, :] = full[a]

    def chunks(src, out):
        r = out.shape[1]
        for a in range(group):
            out[a] = src[a * r : (a + 1) * r, :]

    chunks(work, g_src)
    s1 = scatter_start(0, g_src, g_recv)
    for k, (exists, _, _, _, land) in enumerate(sides):
        @pl.when(exists)
        def _():
            halo_copy(k).start()

        @pl.when(jnp.logical_not(exists))
        def _():
            land[...] = jnp.zeros(land.shape, F32)
    s2 = plane_start(0, s1, g_src, g_recv, g_z)
    s3 = gather_start(0, s2, g_z, g_full)
    gather_end(s3, g_full, work)
    factorize(work, upper, inv_a)
    factor_ref[...] = upper[...] / math.sqrt(all_cells)

    for k, (exists, _, _, _, _) in enumerate(sides):
        @pl.when(exists)
        def _():
            halo_copy(k).wait_send()
            halo_copy(k ^ 1).wait_recv()
    first_inv = inv_a[...].T

    def basis_step(i, carry):
        rows = y_ref[pl.ds(i * 4, 4)].reshape(4 * by * bz, w)
        pad[pl.ds(i * 4 + 1, 4), 1 : by + 1] = mm(rows, first_inv).reshape(4, by, bz, w)
        return carry

    lax.fori_loop(0, bx // 4, basis_step, 0)
    for side, at in ((0, 0), (1, bx + 1)):
        pad[at, 1 : by + 1] = mm(halo_x[side].reshape(by * bz, w), first_inv).reshape(by, bz, w)
    for side, at in ((0, 0), (1, by + 1)):
        pad[1 : bx + 1, at] = mm(halo_y[side].reshape(bx * bz, w), first_inv).reshape(bx, bz, w)

    zero = jnp.zeros((by, 1, w), F32)

    def near_of(x):
        q = pad[x + 1, 1 : by + 1]
        near = pad[x, 1 : by + 1] + pad[x + 2, 1 : by + 1]
        near = near + pad[x + 1, 0:by] + pad[x + 1, 2 : by + 2]
        near = near + jnp.concatenate([q[:, 1:], zero], axis=1)
        near = near + jnp.concatenate([zero, q[:, :-1]], axis=1)
        return q, near

    def field(f, x):
        cell = fields_ref[f, x]
        return jnp.stack([jnp.broadcast_to(cell[:, y : y + 1], (bz, w)) for y in range(by)])

    def flat(v):
        return v.reshape(by * bz, w)

    def gram_two_step(i, total):
        rows = pad[pl.ds(i * 4 + 1, 4), 1 : by + 1].reshape(4 * by * bz, w)
        return total + mm_t(rows, rows)

    h = lax.fori_loop(0, bx // 4, gram_two_step, jnp.zeros((w, w), F32))
    work[...] = h
    chunks(work, h_src)
    t1 = scatter_start(1, h_src, h_recv)

    proj[...] = jnp.zeros(proj.shape, F32)

    def proj_step(x, carry):
        q, near = near_of(x)
        k_block = (6.0 + field(0, x)) * q - near
        c_block = field(1, x) * q
        m_block = field(2, x) * q + near * (1.0 / 12.0)
        wide = jnp.concatenate([flat(k_block), flat(c_block), flat(m_block)], axis=1)
        out = mm_t(flat(q), wide)
        for p in range(3):
            proj[p * w : (p + 1) * w, :] += out[:, p * w : (p + 1) * w]
        return carry

    lax.fori_loop(0, bx, proj_step, 0)
    chunks(proj, p_src)
    r1 = scatter_start(2, p_src, p_recv)
    t2 = plane_start(1, t1, h_src, h_recv, h_z)
    t3 = gather_start(1, t2, h_z, h_full)
    r2 = plane_start(2, r1, p_src, p_recv, p_z)
    gather_end(t3, h_full, work)
    factorize(work, upper, inv_b)
    r3 = gather_start(2, r2, p_z, p_full)

    left = inv_b[...]
    second_inv = left.T
    coeffs = mm(second_inv, ritz_ref[...])

    def vector_step(i, carry):
        rows = pad[pl.ds(i * 2, 2)].reshape(2 * (by + 2) * bz, w)
        pad[pl.ds(i * 2, 2)] = mm(rows, coeffs).reshape(2, by + 2, bz, w)
        return carry

    pad[0, 0] = jnp.zeros((bz, w), F32)
    pad[0, by + 1] = jnp.zeros((bz, w), F32)
    pad[bx + 1, 0] = jnp.zeros((bz, w), F32)
    pad[bx + 1, by + 1] = jnp.zeros((bz, w), F32)
    lax.fori_loop(0, (bx + 2) // 2, vector_step, 0)
    shifts = shifts_ref[...].reshape(1, 1, w)
    squares = shifts * shifts

    def residual_step(x, carry):
        v, near = near_of(x)
        vec_ref[x] = v
        stiff = (6.0 + field(0, x)) * v - near
        res_ref[x] = stiff + field(1, x) * v * shifts + (field(2, x) * v + near * (1.0 / 12.0)) * squares
        return carry

    lax.fori_loop(0, bx, residual_step, 0)

    gather_end(r3, p_full, proj)
    for p, out in enumerate((stiff_ref, damp_ref, mass_ref)):
        out[...] = mm(left, mm(proj[p * w : (p + 1) * w, :], second_inv))
    for copies in (s1, s2, s3, t1, t2, t3, r1, r2, r3):
        for copy in copies:
            copy.wait_send()


def local(sizes, moments, stiffness, damping, density, ritz_coeffs, shifts):
    nx, ny, nz, _ = sizes
    bx, by, bz, w = moments.shape
    group = nx * nz
    fields = jnp.stack([stiffness, damping, density]).transpose(0, 1, 3, 2)
    r = w // group
    q = 3 * w // group
    mat = jax.ShapeDtypeStruct((w, w), F32)
    block = jax.ShapeDtypeStruct(moments.shape, F32)
    square = pltpu.VMEM((w, w), F32)
    vmem = pl.BlockSpec(memory_space=pltpu.VMEM)
    dma = pltpu.SemaphoreType.DMA
    return pl.pallas_call(
        functools.partial(kernel, sizes),
        out_shape=(block, block, mat, mat, mat, mat),
        in_specs=[vmem] * 4,
        out_specs=(vmem,) * 6,
        scratch_shapes=[
            pltpu.VMEM((bx + 2, by + 2, bz, w), F32),
            pltpu.VMEM((2, by, bz, w), F32),
            pltpu.VMEM((2, bx, bz, w), F32),
            square, square, square, square,
            pltpu.VMEM((group, r, w), F32),
            pltpu.VMEM((group, r, w), F32),
            pltpu.VMEM((ny, r, w), F32),
            pltpu.VMEM((group, r, w), F32),
            pltpu.VMEM((group, r, w), F32),
            pltpu.VMEM((ny, r, w), F32),
            pltpu.VMEM((group, r, w), F32),
            pltpu.VMEM((group, q, w), F32),
            pltpu.VMEM((group, q, w), F32),
            pltpu.VMEM((ny, q, w), F32),
            pltpu.VMEM((group, q, w), F32),
            pltpu.VMEM((group, r, w), F32),
            pltpu.VMEM((3 * w, w), F32),
            dma((4,)), dma((4,)),
            dma((3, group - 1)), dma((3, group - 1)),
            dma((3, ny - 1)), dma((3, ny - 1)),
            dma((3, group - 1)), dma((3, group - 1)),
        ],
        compiler_params=pltpu.CompilerParams(
            collective_id=0, has_side_effects=True, vmem_limit_bytes=48 << 20
        ),
    )(moments, fields, ritz_coeffs, shifts.reshape(1, w))


def solution(mesh):
    nx, ny, nz = (mesh.shape[a] for a in ("gx", "gy", "gz"))

    def call(moments, *rest):
        cells = moments.shape[0] * moments.shape[1] * moments.shape[2]
        body = functools.partial(local, (nx, ny, nz, cells * nx * ny * nz))
        return body(moments, *rest)

    cube = P("gx", ("gy", "gz"), None)
    block = P("gx", ("gy", "gz"), None, None)
    return jax.shard_map(
        call,
        mesh=mesh,
        in_specs=(block, cube, cube, cube, P(), P()),
        out_specs=(block, block, P(), P(), P(), P()),
        check_vma=False,
    )
```

```python
import functools
import math
import jax
import jax.numpy as jnp
from jax import lax
from jax.experimental import pallas as pl
from jax.experimental.pallas import tpu as pltpu
from jax.sharding import PartitionSpec as P

MESH = pl.DeviceIdType.MESH
HI = lax.Precision.HIGHEST
F32 = jnp.float32
BF16 = jnp.bfloat16
BLK = 16


def mm(a, b):
    return lax.dot_general(a, b, (((1,), (0,)), ((), ())), precision=HI, preferred_element_type=F32)


def mm_t(a, b):
    return lax.dot_general(a, b, (((0,), (0,)), ((), ())), precision=HI, preferred_element_type=F32)


def split(x):
    high = x.astype(BF16)
    return high, (x - high.astype(F32)).astype(BF16)


def split3(x):
    high = x.astype(BF16)
    rest = x - high.astype(F32)
    mid = rest.astype(BF16)
    return high, mid, (rest - mid.astype(F32)).astype(BF16)


def dot_t(a, b):
    return lax.dot_general(a, b, (((0,), (0,)), ((), ())), preferred_element_type=F32)


def dot(a, b):
    return lax.dot_general(a, b, (((1,), (0,)), ((), ())), preferred_element_type=F32)


def rank_update(a, b):
    ah, am, al = split3(a)
    bh, bm, bl = split3(b)
    left = jnp.concatenate([ah, am, ah, am, ah, al], axis=0)
    right = jnp.concatenate([bh, bh, bm, bm, bl, bh], axis=0)
    return dot_t(left, right)


def coeff_tile(c):
    high, low = split(c)
    return jnp.concatenate(
        [jnp.concatenate([high, low], axis=1), jnp.concatenate([high, jnp.zeros_like(high)], axis=1)], axis=0
    )


def mm_three(rows, tile):
    w = rows.shape[1]
    out = dot(jnp.concatenate(split(rows), axis=1), tile)
    return out[:, :w] + out[:, w:]


def inv_tiles(c):
    high, mid, low = split3(c)
    pair = jnp.concatenate([high, mid], axis=1)
    return jnp.concatenate([pair, pair], axis=0), jnp.concatenate([low, high], axis=0)


def mm_six(rows, tiles):
    w = rows.shape[1]
    high, mid, low = split3(rows)
    one = dot(jnp.concatenate([high, mid], axis=1), tiles[0])
    two = dot(jnp.concatenate([high, low], axis=1), tiles[1])
    return (two + one[:, w:]) + one[:, :w]


def stencil(pad, x, by, zero):
    q = pad[x + 1, 1 : by + 1]
    near = pad[x, 1 : by + 1] + pad[x + 2, 1 : by + 1]
    near = near + pad[x + 1, 0:by] + pad[x + 1, 2 : by + 2]
    near = near + jnp.concatenate([q[:, 1:], zero], axis=1)
    near = near + jnp.concatenate([zero, q[:, :-1]], axis=1)
    return q, near


def field(cells, f, dx, by, bz, w):
    part = cells[f * bz : (f + 1) * bz]
    return jnp.stack([jnp.broadcast_to(part[:, dx * by + y : dx * by + y + 1], (bz, w)) for y in range(by)])


def factorize(work, upper, inverse):
    n = work.shape[0]
    lane = lax.broadcasted_iota(jnp.int32, (BLK, n), 1)
    sub = lax.broadcasted_iota(jnp.int32, (BLK, n), 0)
    lane_all = lax.broadcasted_iota(jnp.int32, (n, n), 1)

    def block(jb, carry):
        first = pl.multiple_of(jb * BLK, BLK)
        rows = work[pl.ds(first, BLK), :]
        cols = [
            jnp.broadcast_to(
                jnp.sum(jnp.where(lane == first + k, rows, 0.0), axis=1, keepdims=True), (BLK, n)
            )
            for k in range(BLK)
        ]
        u = jnp.where(lane >= first, rows, 0.0)
        e = jnp.where(lane < first, rows, jnp.where(lane == first + sub, 1.0, 0.0))
        pivots = jnp.zeros((BLK, n), F32)
        for s in range(BLK):
            pivot = jnp.broadcast_to(cols[s][s : s + 1], (BLK, n))
            pivots = jnp.where(sub == s, pivot, pivots)
            if s == BLK - 1:
                break
            m = jnp.where(sub > s, cols[s] / pivot, 0.0)
            for k in range(s + 1, BLK):
                cols[k] = cols[k] - m * cols[k][s : s + 1]
            u = u - m * u[s : s + 1]
            e = e - m * e[s : s + 1]
        scale = 1.0 / jnp.sqrt(pivots)
        u = jnp.where(lane >= first + sub, u * scale, 0.0)
        e = e * scale
        upper[pl.ds(first, BLK), :] = u
        inverse[pl.ds(first, BLK), :] = e
        beyond = jnp.where(lane >= first + BLK, u, 0.0)
        panel = (lane_all >= first) & (lane_all < first + BLK)
        work[...] = jnp.where(panel, 0.0, work[...]) - rank_update(beyond, beyond + e)
        return carry

    lax.fori_loop(0, n // BLK, block, 0)


def kernel(
    sizes,
    y_hbm, stiff_in, damp_in, dens_in, ritz_ref,
    pad, cells_ref, proj, inv_b, factor_ref,
    y_ref, halo_x, halo_y, work, upper, inv_a,
    g_src, g_recv, g_z, g_full, h_recv, h_z, h_full, p_src, p_recv, p_z, p_full, h_src, load_sem,
    halo_send, halo_got, a_send, a_got, z_send, z_got, b_send, b_got,
):
    nx, ny, nz, all_cells = sizes
    bx, by, bz, w = y_ref.shape
    group = nx * nz
    ix, iy, iz = lax.axis_index("gx"), lax.axis_index("gy"), lax.axis_index("gz")
    mine = ix * nz + iz
    line = iy * nz + iz

    def group_id(a):
        return (lax.div(a, nz), iy, lax.rem(a, nz))

    def line_id(a):
        return (ix, lax.div(a, nz), lax.rem(a, nz))

    sides = [
        (ix > 0, (ix - 1, iy, iz), y_ref.at[0], halo_x.at[1], halo_x.at[0]),
        (ix < nx - 1, (ix + 1, iy, iz), y_ref.at[bx - 1], halo_x.at[0], halo_x.at[1]),
        (line > 0, line_id(line - 1), y_ref.at[:, 0], halo_y.at[1], halo_y.at[0]),
        (line < ny * nz - 1, line_id(line + 1), y_ref.at[:, by - 1], halo_y.at[0], halo_y.at[1]),
    ]
    peers = [lax.rem(mine + d, group) for d in range(1, group)]
    planes = [lax.rem(iy + d, ny) for d in range(1, ny)]

    parts = 4
    px = bx // parts
    loads = [
        pltpu.make_async_copy(y_hbm.at[pl.ds(i * px, px)], y_ref.at[pl.ds(i * px, px)], load_sem.at[i])
        for i in range(parts)
    ]
    for load in loads:
        load.start()

    barrier = pltpu.get_barrier_semaphore()
    for peer in peers:
        pl.semaphore_signal(barrier, inc=1, device_id=group_id(peer), device_id_type=MESH)
    for plane in planes:
        pl.semaphore_signal(barrier, inc=1, device_id=(ix, plane, iz), device_id_type=MESH)
    for exists, device, _, _, _ in sides:
        @pl.when(exists)
        def _():
            pl.semaphore_signal(barrier, inc=1, device_id=device, device_id_type=MESH)

    total = jnp.zeros((w, w), F32)
    for i in range(parts):
        loads[i].wait()
        rows = y_ref[i * px : (i + 1) * px].reshape(px * by * bz, w)
        total = total + mm_t(rows, rows)
    work[...] = total

    empty = jnp.zeros((bx * by, w - 3 * bz), F32)
    cells_ref[...] = jnp.concatenate([stiff_in[...], damp_in[...], dens_in[...], empty], axis=1).T

    beside = sum(exists.astype(jnp.int32) for exists, _, _, _, _ in sides)
    pl.semaphore_wait(barrier, group - 1 + ny - 1 + beside)

    def halo_copy(k):
        _, device, src, dst, _ = sides[k]
        other = k ^ 1
        return pltpu.make_async_remote_copy(
            src_ref=src, dst_ref=dst, send_sem=halo_send.at[k], recv_sem=halo_got.at[other],
            device_id=device, device_id_type=MESH,
        )

    def scatter_start(slot, src, recv):
        copies = []
        for d, peer in enumerate(peers):
            copy = pltpu.make_async_remote_copy(
                src_ref=src.at[peer], dst_ref=recv.at[d], send_sem=a_send.at[slot, d],
                recv_sem=a_got.at[slot, d], device_id=group_id(peer), device_id_type=MESH,
            )
            copy.start()
            copies.append(copy)
        return copies

    def plane_start(slot, copies, src, recv, z):
        for copy in copies:
            copy.wait_recv()
        total = src[mine]
        for d in range(group - 1):
            total = total + recv[d]
        z[iy] = total
        after = []
        for d, plane in enumerate(planes):
            copy = pltpu.make_async_remote_copy(
                src_ref=z.at[iy], dst_ref=z.at[iy], send_sem=z_send.at[slot, d],
                recv_sem=z_got.at[slot, d], device_id=(ix, plane, iz), device_id_type=MESH,
            )
            copy.start()
            after.append(copy)
        return after

    def gather_start(slot, copies, z, full):
        for copy in copies:
            copy.wait_recv()
        total = z[0]
        for d in range(1, ny):
            total = total + z[d]
        full[mine] = total
        after = []
        for d, peer in enumerate(peers):
            copy = pltpu.make_async_remote_copy(
                src_ref=full.at[mine], dst_ref=full.at[mine], send_sem=b_send.at[slot, d],
                recv_sem=b_got.at[slot, d], device_id=group_id(peer), device_id_type=MESH,
            )
            copy.start()
            after.append(copy)
        return after

    def gather_end(copies, full, out):
        for copy in copies:
            copy.wait_recv()
        r = full.shape[1]
        for a in range(group):
            out[a * r : (a + 1) * r, :] = full[a]

    def chunks(src, out):
        r = out.shape[1]
        for a in range(group):
            out[a] = src[a * r : (a + 1) * r, :]

    chunks(work, g_src)
    s1 = scatter_start(0, g_src, g_recv)
    for k, (exists, _, _, _, land) in enumerate(sides):
        @pl.when(exists)
        def _():
            halo_copy(k).start()

        @pl.when(jnp.logical_not(exists))
        def _():
            land[...] = jnp.zeros(land.shape, F32)
    s2 = plane_start(0, s1, g_src, g_recv, g_z)
    s3 = gather_start(0, s2, g_z, g_full)
    gather_end(s3, g_full, work)
    factorize(work, upper, inv_a)
    factor_ref[...] = upper[...] / math.sqrt(all_cells)

    for k, (exists, _, _, _, _) in enumerate(sides):
        @pl.when(exists)
        def _():
            halo_copy(k).wait_send()
            halo_copy(k ^ 1).wait_recv()
    tiles = inv_tiles(inv_a[...].T)

    def basis_step(i, carry):
        rows = y_ref[pl.ds(i * 4, 4)].reshape(4 * by * bz, w)
        pad[pl.ds(i * 4 + 1, 4), 1 : by + 1] = mm_six(rows, tiles).reshape(4, by, bz, w)
        return carry

    def gram_two_step(i, total):
        rows = pad[pl.ds(i * 4 + 1, 4), 1 : by + 1].reshape(4 * by * bz, w)
        high, low = split(rows)
        return total + dot_t(high, jnp.concatenate([high, low], axis=1))

    lax.fori_loop(0, bx // 4, basis_step, 0)
    pair = lax.fori_loop(0, bx // 4, gram_two_step, jnp.zeros((w, 2 * w), F32))
    cross = pair[:, w:]
    work[...] = pair[:, :w] + (cross + cross.T)
    chunks(work, h_src)
    t1 = scatter_start(1, h_src, h_recv)

    for side, at in ((0, 0), (1, bx + 1)):
        pad[at, 1 : by + 1] = mm_six(halo_x[side].reshape(by * bz, w), tiles).reshape(by, bz, w)
    for side, at in ((0, 0), (1, by + 1)):
        pad[1 : bx + 1, at] = mm_six(halo_y[side].reshape(bx * bz, w), tiles).reshape(bx, bz, w)
    for at_x in (0, bx + 1):
        for at_y in (0, by + 1):
            pad[at_x, at_y] = jnp.zeros((bz, w), F32)

    zero = jnp.zeros((by, 1, w), F32)
    lanes = bx * by
    proj[...] = jnp.zeros(proj.shape, F32)

    def proj_step(i, carry):
        cells = pltpu.roll(cells_ref[0 : 3 * bz, :], lax.rem(lanes - i * 2 * by, lanes), 1)
        qs, wides = [], []
        for dx in range(2):
            q, near = stencil(pad, i * 2 + dx, by, zero)
            k_block = (6.0 + field(cells, 0, dx, by, bz, w)) * q - near
            c_block = field(cells, 1, dx, by, bz, w) * q
            m_block = field(cells, 2, dx, by, bz, w) * q + near * (1.0 / 12.0)
            qs.append(q.reshape(by * bz, w))
            wides.append(jnp.concatenate([v.reshape(by * bz, w) for v in (k_block, c_block, m_block)], axis=1))
        qh, ql = split(jnp.concatenate(qs, axis=0))
        vh, vl = split(jnp.concatenate(wides, axis=0))
        out = dot_t(ql, vh) + dot_t(qh, vl) + dot_t(qh, vh)
        for p in range(3):
            proj[p * w : (p + 1) * w, :] += out[:, p * w : (p + 1) * w]
        return carry

    third = bx // 2 // 3
    lax.fori_loop(0, third, proj_step, 0)
    t2 = plane_start(1, t1, h_src, h_recv, h_z)
    lax.fori_loop(third, 2 * third, proj_step, 0)
    t3 = gather_start(1, t2, h_z, h_full)
    lax.fori_loop(2 * third, bx // 2, proj_step, 0)
    chunks(proj, p_src)
    r1 = scatter_start(2, p_src, p_recv)
    gather_end(t3, h_full, work)
    factorize(work, upper, inv_b)
    r2 = plane_start(2, r1, p_src, p_recv, p_z)
    tile = coeff_tile(mm(inv_b[...].T, ritz_ref[...]))

    def vector_step(i, carry):
        rows = pad[pl.ds(i * 2, 2)].reshape(2 * (by + 2) * bz, w)
        pad[pl.ds(i * 2, 2)] = mm_three(rows, tile).reshape(2, by + 2, bz, w)
        return carry

    lax.fori_loop(0, (bx + 2) // 2, vector_step, 0)
    r3 = gather_start(2, r2, p_z, p_full)
    for copies in (s1, s2, s3, t1, t2, t3, r1, r2):
        for copy in copies:
            copy.wait_send()
    gather_end(r3, p_full, proj)
    for copy in r3:
        copy.wait_send()


def finish(
    pad, cells_ref, proj, inv_ref, factor_in, shifts_ref,
    vec_ref, res_ref, stiff_ref, damp_ref, mass_ref, factor_ref,
):
    step = pl.program_id(0)
    px, by, bz, w = vec_ref.shape
    lanes = cells_ref.shape[1]
    zero = jnp.zeros((by, 1, w), F32)
    cells = pltpu.roll(cells_ref[0 : 3 * bz, :], lax.rem(lanes - step * px * by, lanes), 1)
    shifts = shifts_ref[...].reshape(1, 1, w)
    squares = shifts * shifts
    near_scale = squares * (1.0 / 12.0) - 1.0
    for dx in range(px):
        v, near = stencil(pad, step * px + dx, by, zero)
        vec_ref[dx] = v
        diag = (6.0 + field(cells, 0, dx, by, bz, w)) + field(cells, 1, dx, by, bz, w) * shifts
        diag = diag + field(cells, 2, dx, by, bz, w) * squares
        res_ref[dx] = diag * v + near_scale * near

    @pl.when(step == 0)
    def _():
        left = inv_ref[...]
        mid = mm(proj[...], left.T)
        out = mm(left, jnp.concatenate([mid[p * w : (p + 1) * w] for p in range(3)], axis=1))
        stiff_ref[...] = out[:, :w]
        damp_ref[...] = out[:, w : 2 * w]
        mass_ref[...] = out[:, 2 * w :]
        factor_ref[...] = factor_in[...]


def local(sizes, moments, stiffness, damping, density, ritz_coeffs, shifts):
    nx, ny, nz, _ = sizes
    bx, by, bz, w = moments.shape
    group = nx * nz
    flat = [f.reshape(bx * by, bz) for f in (stiffness, damping, density)]
    r = w // group
    q = 3 * w // group
    mat = jax.ShapeDtypeStruct((w, w), F32)
    block = jax.ShapeDtypeStruct(moments.shape, F32)
    square = pltpu.VMEM((w, w), F32)
    vmem = pl.BlockSpec(memory_space=pltpu.VMEM)
    dma = pltpu.SemaphoreType.DMA
    padded = (bx + 2, by + 2, bz, w)
    shared = pl.pallas_call(
        functools.partial(kernel, sizes),
        out_shape=(
            jax.ShapeDtypeStruct(padded, F32), mat, jax.ShapeDtypeStruct((3 * w, w), F32), mat, mat,
        ),
        in_specs=[pl.BlockSpec(memory_space=pl.ANY)] + [vmem] * 4,
        out_specs=(vmem,) * 5,
        scratch_shapes=[
            pltpu.VMEM(moments.shape, F32),
            pltpu.VMEM((2, by, bz, w), F32),
            pltpu.VMEM((2, bx, bz, w), F32),
            square, square, square,
            pltpu.VMEM((group, r, w), F32),
            pltpu.VMEM((group, r, w), F32),
            pltpu.VMEM((ny, r, w), F32),
            pltpu.VMEM((group, r, w), F32),
            pltpu.VMEM((group, r, w), F32),
            pltpu.VMEM((ny, r, w), F32),
            pltpu.VMEM((group, r, w), F32),
            pltpu.VMEM((group, q, w), F32),
            pltpu.VMEM((group, q, w), F32),
            pltpu.VMEM((ny, q, w), F32),
            pltpu.VMEM((group, q, w), F32),
            pltpu.VMEM((group, r, w), F32),
            dma((4,)),
            dma((4,)), dma((4,)),
            dma((3, group - 1)), dma((3, group - 1)),
            dma((3, ny - 1)), dma((3, ny - 1)),
            dma((3, group - 1)), dma((3, group - 1)),
        ],
        compiler_params=pltpu.CompilerParams(
            collective_id=0, has_side_effects=True, vmem_limit_bytes=24 << 20
        ),
    )(moments, *flat, ritz_coeffs)
    px = 4
    tile = pl.BlockSpec((px, by, bz, w), lambda i: (i, 0, 0, 0))
    whole = pl.BlockSpec((w, w), lambda i: (0, 0))
    return pl.pallas_call(
        finish,
        grid=(bx // px,),
        out_shape=(block, block, mat, mat, mat, mat),
        in_specs=[vmem] * 6,
        out_specs=(tile, tile, whole, whole, whole, whole),
        compiler_params=pltpu.CompilerParams(vmem_limit_bytes=24 << 20),
    )(*shared, shifts.reshape(1, w))


def solution(mesh):
    nx, ny, nz = (mesh.shape[a] for a in ("gx", "gy", "gz"))

    def call(moments, *rest):
        cells = moments.shape[0] * moments.shape[1] * moments.shape[2]
        body = functools.partial(local, (nx, ny, nz, cells * nx * ny * nz))
        return body(moments, *rest)

    cube = P("gx", ("gy", "gz"), None)
    block = P("gx", ("gy", "gz"), None, None)
    return jax.shard_map(
        call,
        mesh=mesh,
        in_specs=(block, cube, cube, cube, P(), P()),
        out_specs=(block, block, P(), P(), P(), P()),
        check_vma=False,
    )
```

```python
import functools
import math
import jax
import jax.numpy as jnp
from jax import lax
from jax.experimental import pallas as pl
from jax.experimental.pallas import tpu as pltpu
from jax.sharding import PartitionSpec as P

MESH = pl.DeviceIdType.MESH
HI = lax.Precision.HIGHEST
F32 = jnp.float32
BF16 = jnp.bfloat16
BLK = 16


def mm(a, b):
    return lax.dot_general(a, b, (((1,), (0,)), ((), ())), precision=HI, preferred_element_type=F32)


def mm_t(a, b):
    return lax.dot_general(a, b, (((0,), (0,)), ((), ())), precision=HI, preferred_element_type=F32)


def split(x):
    high = x.astype(BF16)
    return high, (x - high.astype(F32)).astype(BF16)


def split3(x):
    high = x.astype(BF16)
    rest = x - high.astype(F32)
    mid = rest.astype(BF16)
    return high, mid, (rest - mid.astype(F32)).astype(BF16)


def dot_t(a, b):
    return lax.dot_general(a, b, (((0,), (0,)), ((), ())), preferred_element_type=F32)


def dot(a, b):
    return lax.dot_general(a, b, (((1,), (0,)), ((), ())), preferred_element_type=F32)


def rank_update(a, b):
    ah, am, al = split3(a)
    bh, bm, bl = split3(b)
    left = jnp.concatenate([ah, am, ah, am, ah, al], axis=0)
    right = jnp.concatenate([bh, bh, bm, bm, bl, bh], axis=0)
    return dot_t(left, right)


def coeff_tile(c):
    high, low = split(c)
    return jnp.concatenate(
        [jnp.concatenate([high, low], axis=1), jnp.concatenate([high, jnp.zeros_like(high)], axis=1)], axis=0
    )


def mm_three(rows, tile):
    w = rows.shape[1]
    out = dot(jnp.concatenate(split(rows), axis=1), tile)
    return out[:, :w] + out[:, w:]


def inv_tiles(c):
    high, mid, low = split3(c)
    pair = jnp.concatenate([high, mid], axis=1)
    return jnp.concatenate([pair, pair], axis=0), jnp.concatenate([low, high], axis=0)


def mm_six(rows, tiles):
    w = rows.shape[1]
    high, mid, low = split3(rows)
    one = dot(jnp.concatenate([high, mid], axis=1), tiles[0])
    two = dot(jnp.concatenate([high, low], axis=1), tiles[1])
    return (two + one[:, w:]) + one[:, :w]


def stencil(pad, x, by, zero):
    q = pad[x + 1, 1 : by + 1]
    near = pad[x, 1 : by + 1] + pad[x + 2, 1 : by + 1]
    near = near + pad[x + 1, 0:by] + pad[x + 1, 2 : by + 2]
    near = near + jnp.concatenate([q[:, 1:], zero], axis=1)
    near = near + jnp.concatenate([zero, q[:, :-1]], axis=1)
    return q, near


def field(cells, f, dx, by, bz, w):
    part = cells[f * bz : (f + 1) * bz]
    return jnp.stack([jnp.broadcast_to(part[:, dx * by + y : dx * by + y + 1], (bz, w)) for y in range(by)])


def factorize(work, upper, inverse, between=None):
    n = work.shape[0]
    lane = lax.broadcasted_iota(jnp.int32, (BLK, n), 1)
    sub = lax.broadcasted_iota(jnp.int32, (BLK, n), 0)
    lane_all = lax.broadcasted_iota(jnp.int32, (n, n), 1)

    def block(jb, carry):
        first = pl.multiple_of(jb * BLK, BLK)
        rows = work[pl.ds(first, BLK), :]
        cols = [
            jnp.broadcast_to(
                jnp.sum(jnp.where(lane == first + k, rows, 0.0), axis=1, keepdims=True), (BLK, n)
            )
            for k in range(BLK)
        ]
        u = jnp.where(lane >= first, rows, 0.0)
        e = jnp.where(lane < first, rows, jnp.where(lane == first + sub, 1.0, 0.0))
        pivots = jnp.zeros((BLK, n), F32)
        for s in range(BLK):
            pivot = jnp.broadcast_to(cols[s][s : s + 1], (BLK, n))
            pivots = jnp.where(sub == s, pivot, pivots)
            if s == BLK - 1:
                break
            m = jnp.where(sub > s, cols[s] / pivot, 0.0)
            for k in range(s + 1, BLK):
                cols[k] = cols[k] - m * cols[k][s : s + 1]
            u = u - m * u[s : s + 1]
            e = e - m * e[s : s + 1]
        scale = 1.0 / jnp.sqrt(pivots)
        u = jnp.where(lane >= first + sub, u * scale, 0.0)
        e = e * scale
        upper[pl.ds(first, BLK), :] = u
        inverse[pl.ds(first, BLK), :] = e
        beyond = jnp.where(lane >= first + BLK, u, 0.0)
        panel = (lane_all >= first) & (lane_all < first + BLK)
        work[...] = jnp.where(panel, 0.0, work[...]) - rank_update(beyond, beyond + e)
        return carry

    late = n // BLK * 3 // 4
    lax.fori_loop(0, late, block, 0)
    result = between() if between else None
    lax.fori_loop(late, n // BLK, block, 0)
    return result


def kernel(
    sizes,
    y_hbm, stiff_in, damp_in, dens_in, ritz_in,
    pad_out, cells_out, proj_out, inv_out, factor_out,
    pad, cells_ref, proj, inv_b, factor_ref, out_sem,
    y_ref, fields, ritz_ref, halo_x, halo_y, work, upper, inv_a,
    g_src, g_recv, g_z, g_full, h_recv, h_z, h_full, p_src, p_recv, p_z, p_full, h_src, load_sem,
    halo_send, halo_got, a_send, a_got, z_send, z_got, b_send, b_got,
):
    nx, ny, nz, all_cells = sizes
    bx, by, bz, w = y_ref.shape
    group, levels = g_recv.shape[0], g_z.shape[0]
    ix, iy, iz = lax.axis_index("gx"), lax.axis_index("gy"), lax.axis_index("gz")
    mine = ix * nz + iz
    level = iy
    line = iy * nz + iz

    def group_id(a):
        return (lax.div(a, nz), iy, lax.rem(a, nz))

    def line_id(a):
        return (ix, lax.div(a, nz), lax.rem(a, nz))

    sides = [
        (ix > 0, (ix - 1, iy, iz), y_ref.at[0], halo_x.at[1], halo_x.at[0]),
        (ix < nx - 1, (ix + 1, iy, iz), y_ref.at[bx - 1], halo_x.at[0], halo_x.at[1]),
        (line > 0, line_id(line - 1), y_ref.at[:, 0], halo_y.at[1], halo_y.at[0]),
        (line < ny * nz - 1, line_id(line + 1), y_ref.at[:, by - 1], halo_y.at[0], halo_y.at[1]),
    ]
    peers = [lax.rem(mine + d, group) for d in range(1, group)]
    planes = [lax.rem(iy + d, ny) for d in range(1, levels)]

    parts = 4
    px = bx // parts
    loads = [
        pltpu.make_async_copy(y_hbm.at[pl.ds(i * px, px)], y_ref.at[pl.ds(i * px, px)], load_sem.at[i])
        for i in range(parts)
    ]
    for f, src in enumerate((stiff_in, damp_in, dens_in)):
        loads.append(pltpu.make_async_copy(src, fields.at[f], load_sem.at[parts + f]))
    loads.append(pltpu.make_async_copy(ritz_in, ritz_ref, load_sem.at[parts + 3]))
    for load in loads:
        load.start()

    barrier = pltpu.get_barrier_semaphore()
    for peer in peers:
        pl.semaphore_signal(barrier, inc=1, device_id=group_id(peer), device_id_type=MESH)
    for plane in planes:
        pl.semaphore_signal(barrier, inc=1, device_id=(ix, plane, iz), device_id_type=MESH)
    for exists, device, _, _, _ in sides:
        @pl.when(exists)
        def _():
            pl.semaphore_signal(barrier, inc=1, device_id=device, device_id_type=MESH)

    total = jnp.zeros((w, w), F32)
    for i in range(parts):
        loads[i].wait()
        rows = y_ref[i * px : (i + 1) * px].reshape(px * by * bz, w)
        total = total + mm_t(rows, rows)
    work[...] = total

    empty = jnp.zeros((bx * by, w - 3 * bz), F32)
    for load in loads[parts:]:
        load.wait()
    cells_ref[...] = jnp.concatenate([fields[0], fields[1], fields[2], empty], axis=1).T
    stores = [
        pltpu.make_async_copy(a, b, out_sem.at[i])
        for i, (a, b) in enumerate((
            (cells_ref, cells_out), (factor_ref, factor_out), (inv_b, inv_out), (pad, pad_out), (proj, proj_out),
        ))
    ]
    stores[0].start()

    beside = sum(exists.astype(jnp.int32) for exists, _, _, _, _ in sides)
    pl.semaphore_wait(barrier, group - 1 + levels - 1 + beside)

    def halo_copy(k):
        _, device, src, dst, _ = sides[k]
        other = k ^ 1
        return pltpu.make_async_remote_copy(
            src_ref=src, dst_ref=dst, send_sem=halo_send.at[k], recv_sem=halo_got.at[other],
            device_id=device, device_id_type=MESH,
        )

    def scatter_start(slot, src, recv):
        copies = []
        for d, peer in enumerate(peers):
            copy = pltpu.make_async_remote_copy(
                src_ref=src.at[peer], dst_ref=recv.at[d], send_sem=a_send.at[slot, d],
                recv_sem=a_got.at[slot, d], device_id=group_id(peer), device_id_type=MESH,
            )
            copy.start()
            copies.append(copy)
        return copies

    def plane_start(slot, copies, src, recv, z):
        for copy in copies:
            copy.wait_recv()
        total = src[mine]
        for d in range(group - 1):
            total = total + recv[d]
        z[level] = total
        after = []
        for d, plane in enumerate(planes):
            copy = pltpu.make_async_remote_copy(
                src_ref=z.at[level], dst_ref=z.at[level], send_sem=z_send.at[slot, d],
                recv_sem=z_got.at[slot, d], device_id=(ix, plane, iz), device_id_type=MESH,
            )
            copy.start()
            after.append(copy)
        return after

    def gather_start(slot, copies, z, full):
        for copy in copies:
            copy.wait_recv()
        total = z[0]
        for d in range(1, levels):
            total = total + z[d]
        full[mine] = total
        after = []
        for d, peer in enumerate(peers):
            copy = pltpu.make_async_remote_copy(
                src_ref=full.at[mine], dst_ref=full.at[mine], send_sem=b_send.at[slot, d],
                recv_sem=b_got.at[slot, d], device_id=group_id(peer), device_id_type=MESH,
            )
            copy.start()
            after.append(copy)
        return after

    def gather_end(copies, full, out):
        for copy in copies:
            copy.wait_recv()
        r = full.shape[1]
        for a in range(group):
            out[a * r : (a + 1) * r, :] = full[a]

    def chunks(src, out):
        r = out.shape[1]
        for a in range(group):
            out[a] = src[a * r : (a + 1) * r, :]

    chunks(work, g_src)
    s1 = scatter_start(0, g_src, g_recv)
    s2 = plane_start(0, s1, g_src, g_recv, g_z)
    s3 = gather_start(0, s2, g_z, g_full)
    gather_end(s3, g_full, work)
    for k, (exists, _, _, _, land) in enumerate(sides):
        @pl.when(exists)
        def _():
            halo_copy(k).start()

        @pl.when(jnp.logical_not(exists))
        def _():
            land[...] = jnp.zeros(land.shape, F32)
    factorize(work, upper, inv_a)
    factor_ref[...] = upper[...] / math.sqrt(all_cells)
    stores[1].start()

    for k, (exists, _, _, _, _) in enumerate(sides):
        @pl.when(exists)
        def _():
            halo_copy(k).wait_send()
            halo_copy(k ^ 1).wait_recv()
    tiles = inv_tiles(inv_a[...].T)

    def basis_step(i, carry):
        rows = y_ref[pl.ds(i * 4, 4)].reshape(4 * by * bz, w)
        pad[pl.ds(i * 4 + 1, 4), 1 : by + 1] = mm_six(rows, tiles).reshape(4, by, bz, w)
        return carry

    def gram_two_step(i, total):
        rows = pad[pl.ds(i * 4 + 1, 4), 1 : by + 1].reshape(4 * by * bz, w)
        high, low = split(rows)
        return total + dot_t(high, jnp.concatenate([high, low], axis=1))

    lax.fori_loop(0, bx // 4, basis_step, 0)
    pair = lax.fori_loop(0, bx // 4, gram_two_step, jnp.zeros((w, 2 * w), F32))
    cross = pair[:, w:]
    work[...] = pair[:, :w] + (cross + cross.T)
    chunks(work, h_src)
    t1 = scatter_start(1, h_src, h_recv)

    for side, at in ((0, 0), (1, bx + 1)):
        pad[at, 1 : by + 1] = mm_six(halo_x[side].reshape(by * bz, w), tiles).reshape(by, bz, w)
    for side, at in ((0, 0), (1, by + 1)):
        pad[1 : bx + 1, at] = mm_six(halo_y[side].reshape(bx * bz, w), tiles).reshape(bx, bz, w)
    for at_x in (0, bx + 1):
        for at_y in (0, by + 1):
            pad[at_x, at_y] = jnp.zeros((bz, w), F32)

    zero = jnp.zeros((by, 1, w), F32)
    lanes = bx * by
    proj[...] = jnp.zeros(proj.shape, F32)

    def proj_step(i, carry):
        cells = pltpu.roll(cells_ref[0 : 3 * bz, :], lax.rem(lanes - i * 2 * by, lanes), 1)
        qs, wides = [], []
        for dx in range(2):
            q, near = stencil(pad, i * 2 + dx, by, zero)
            k_block = (6.0 + field(cells, 0, dx, by, bz, w)) * q - near
            c_block = field(cells, 1, dx, by, bz, w) * q
            m_block = field(cells, 2, dx, by, bz, w) * q + near * (1.0 / 12.0)
            qs.append(q.reshape(by * bz, w))
            wides.append(jnp.concatenate([v.reshape(by * bz, w) for v in (k_block, c_block, m_block)], axis=1))
        qh, ql = split(jnp.concatenate(qs, axis=0))
        vh, vl = split(jnp.concatenate(wides, axis=0))
        out = dot_t(ql, vh) + dot_t(qh, vl) + dot_t(qh, vh)
        for p in range(3):
            proj[p * w : (p + 1) * w, :] += out[:, p * w : (p + 1) * w]
        return carry

    third = bx // 2 // 3
    lax.fori_loop(0, third, proj_step, 0)
    t2 = plane_start(1, t1, h_src, h_recv, h_z)
    lax.fori_loop(third, 2 * third, proj_step, 0)
    t3 = gather_start(1, t2, h_z, h_full)
    lax.fori_loop(2 * third, bx // 2, proj_step, 0)
    chunks(proj, p_src)
    r1 = scatter_start(2, p_src, p_recv)
    gather_end(t3, h_full, work)
    r2 = factorize(work, upper, inv_b, lambda: plane_start(2, r1, p_src, p_recv, p_z))
    stores[2].start()
    r3 = gather_start(2, r2, p_z, p_full)
    tile = coeff_tile(mm(inv_b[...].T, ritz_ref[...]))

    def vector_step(i, carry):
        rows = pad[pl.ds(i * 2, 2)].reshape(2 * (by + 2) * bz, w)
        pad[pl.ds(i * 2, 2)] = mm_three(rows, tile).reshape(2, by + 2, bz, w)
        return carry

    lax.fori_loop(0, (bx + 2) // 2, vector_step, 0)
    stores[3].start()
    for copies in (s1, s2, s3, t1, t2, t3, r1, r2):
        for copy in copies:
            copy.wait_send()
    gather_end(r3, p_full, proj)
    stores[4].start()
    for copy in r3:
        copy.wait_send()
    for store in stores:
        store.wait()


def finish(
    pad_in, cells_in, proj_in, inv_in, factor_in, shifts_in,
    vec_ref, res_ref, stiff_ref, damp_ref, mass_ref, factor_ref,
    pad, cells_ref, proj, inv_ref, shifts_ref, sems,
):
    step = pl.program_id(0)

    def loads():
        pairs = (
            (cells_in, cells_ref), (shifts_in, shifts_ref), (pad_in, pad),
            (proj_in, proj), (inv_in, inv_ref), (factor_in, factor_ref),
        )
        return [pltpu.make_async_copy(a, b, sems.at[i]) for i, (a, b) in enumerate(pairs)]

    @pl.when(step == 0)
    def _():
        for load in loads():
            load.start()
        for load in loads():
            load.wait()

    px, by, bz, w = vec_ref.shape
    lanes = cells_ref.shape[1]
    zero = jnp.zeros((by, 1, w), F32)
    cells = pltpu.roll(cells_ref[0 : 3 * bz, :], lax.rem(lanes - step * px * by, lanes), 1)
    shifts = shifts_ref[...].reshape(1, 1, w)
    squares = shifts * shifts
    near_scale = squares * (1.0 / 12.0) - 1.0
    for dx in range(px):
        v, near = stencil(pad, step * px + dx, by, zero)
        vec_ref[dx] = v
        diag = (6.0 + field(cells, 0, dx, by, bz, w)) + field(cells, 1, dx, by, bz, w) * shifts
        diag = diag + field(cells, 2, dx, by, bz, w) * squares
        res_ref[dx] = diag * v + near_scale * near

    @pl.when(step == 0)
    def _():
        left = inv_ref[...]
        mid = mm(proj[...], left.T)
        out = mm(left, jnp.concatenate([mid[p * w : (p + 1) * w] for p in range(3)], axis=1))
        stiff_ref[...] = out[:, :w]
        damp_ref[...] = out[:, w : 2 * w]
        mass_ref[...] = out[:, 2 * w :]


def local(sizes, moments, stiffness, damping, density, ritz_coeffs, shifts):
    nx, ny, nz, _ = sizes
    bx, by, bz, w = moments.shape
    group, levels = nx * nz, ny
    flat = [f.reshape(bx * by, bz) for f in (stiffness, damping, density)]
    r = w // group
    q = 3 * w // group
    mat = jax.ShapeDtypeStruct((w, w), F32)
    block = jax.ShapeDtypeStruct(moments.shape, F32)
    square = pltpu.VMEM((w, w), F32)
    hbm = pl.BlockSpec(memory_space=pltpu.HBM)
    dma = pltpu.SemaphoreType.DMA
    padded = (bx + 2, by + 2, bz, w)
    shared = pl.pallas_call(
        functools.partial(kernel, sizes),
        out_shape=(
            jax.ShapeDtypeStruct(padded, F32), mat, jax.ShapeDtypeStruct((3 * w, w), F32), mat, mat,
        ),
        in_specs=[hbm] * 5,
        out_specs=(hbm,) * 5,
        scratch_shapes=[
            pltpu.VMEM(padded, F32),
            square,
            pltpu.VMEM((3 * w, w), F32),
            square, square,
            dma((5,)),
            pltpu.VMEM(moments.shape, F32),
            pltpu.VMEM((3, bx * by, bz), F32),
            pltpu.VMEM((w, w), F32),
            pltpu.VMEM((2, by, bz, w), F32),
            pltpu.VMEM((2, bx, bz, w), F32),
            square, square, square,
            pltpu.VMEM((group, r, w), F32),
            pltpu.VMEM((group, r, w), F32),
            pltpu.VMEM((levels, r, w), F32),
            pltpu.VMEM((group, r, w), F32),
            pltpu.VMEM((group, r, w), F32),
            pltpu.VMEM((levels, r, w), F32),
            pltpu.VMEM((group, r, w), F32),
            pltpu.VMEM((group, q, w), F32),
            pltpu.VMEM((group, q, w), F32),
            pltpu.VMEM((levels, q, w), F32),
            pltpu.VMEM((group, q, w), F32),
            pltpu.VMEM((group, r, w), F32),
            dma((8,)),
            dma((4,)), dma((4,)),
            dma((3, group - 1)), dma((3, group - 1)),
            dma((3, max(levels - 1, 1))), dma((3, max(levels - 1, 1))),
            dma((3, group - 1)), dma((3, group - 1)),
        ],
        compiler_params=pltpu.CompilerParams(
            collective_id=0, has_side_effects=True, vmem_limit_bytes=60 << 20
        ),
    )(moments, *flat, ritz_coeffs)
    px = 4
    tile = pl.BlockSpec((px, by, bz, w), lambda i: (i, 0, 0, 0))
    whole = pl.BlockSpec((w, w), lambda i: (0, 0))
    return pl.pallas_call(
        finish,
        grid=(bx // px,),
        out_shape=(block, block, mat, mat, mat, mat),
        in_specs=[hbm] * 6,
        out_specs=(tile, tile, whole, whole, whole, whole),
        scratch_shapes=[
            pltpu.VMEM(padded, F32), square, pltpu.VMEM((3 * w, w), F32), square, pltpu.VMEM((1, w), F32), dma((6,)),
        ],
        compiler_params=pltpu.CompilerParams(vmem_limit_bytes=60 << 20),
    )(*shared, shifts.reshape(1, w))


def solution(mesh):
    nx, ny, nz = (mesh.shape[a] for a in ("gx", "gy", "gz"))

    def call(moments, *rest):
        cells = moments.shape[0] * moments.shape[1] * moments.shape[2]
        body = functools.partial(local, (nx, ny, nz, cells * nx * ny * nz))
        return body(moments, *rest)

    cube = P("gx", ("gy", "gz"), None)
    block = P("gx", ("gy", "gz"), None, None)
    return jax.shard_map(
        call,
        mesh=mesh,
        in_specs=(block, cube, cube, cube, P(), P()),
        out_specs=(block, block, P(), P(), P(), P()),
        check_vma=False,
    )
```
